32 devices in a mesh: seq: 16 (over z, y, x), wa: 2 (over core).
Axes of the slice: x: 2, y: 2, z: 4, core: 2. Of those that a mesh axis runs over, the one named last changes fastest.
Arguments:
- block_input: bfloat16 [16384, 1024], P('seq'), may hold values from -6 to 6
- doc_start: int32 [16384], P('seq'), may hold values from 0 to 16383, as said below
- norm1_gain: bfloat16 [1024], replicated, may hold values from 0.25 to 1.75
- in_weight: bfloat16 [3, 1024, 1024], P(None, 'seq', 'wa'), may hold values from -0.1875 to 0.1875
- conv_taps: bfloat16 [3, 1024], P(None, 'wa'), may hold values from -3 to 3
- out_weight: bfloat16 [1024, 1024], P('wa', 'seq'), may hold values from -0.1875 to 0.1875
- norm2_gain: bfloat16 [1024], replicated, may hold values from 0.25 to 1.75
- gate_weight: bfloat16 [1024, 4608], P('seq', 'wa'), may hold values from -0.1875 to 0.1875
- up_weight: bfloat16 [1024, 4608], P('seq', 'wa'), may hold values from -0.1875 to 0.1875
- down_weight: bfloat16 [4608, 1024], P('wa', 'seq'), may hold values from -0.09375 to 0.09375
- out_grad: bfloat16 [16384, 1024], P('seq'), may hold values from -6 to 6
Outputs:
- block_output: bfloat16 [16384, 1024], P('seq')
- input_grad: float32 [16384, 1024], P('seq')
- norm1_gain_grad: float32 [1024], replicated
- in_weight_grad: float32 [3, 1024, 1024], P(None, 'seq', 'wa')
- conv_taps_grad: float32 [3, 1024], P(None, 'wa')
- out_weight_grad: float32 [1024, 1024], P('wa', 'seq')
- norm2_gain_grad: float32 [1024], replicated
- gate_weight_grad: float32 [1024, 4608], P('seq', 'wa')
- up_weight_grad: float32 [1024, 4608], P('seq', 'wa')
- down_weight_grad: float32 [4608, 1024], P('wa', 'seq')
The draws below stay inside these ranges and needn't reach their ends.
Inputs may be any that keep to these rules, and one draw needn't show every extreme that they name: doc_start[t] is the first token of the document that holds token t: documents are contiguous, doc_start never falls along the stream, doc_start[t] <= t, and doc_start[t] = t where a document begins; documents run across the borders of the seq shards; the first token and the last token of the stream each begin a document.
All inputs are finite; a program needn't handle non-finite values.
Results may differ from the reference program's by a relative error of at most 0.011.
Values may be sent and summed in bfloat16 or wider, within the bound.
No kernel may reach another device: no remote copies, remote signals or barrier semaphores. Data moves between devices by JAX's collectives and lax.ppermute only.
A program may use at most 192 MiB of HBM per device.

```python
import jax
import jax.numpy as jnp
from jax import lax

D = 1024
FF = 4608
KC = 3
TOK_DEV = 1024
TOKENS = 16384


def draw_doc_start(key, part):
    position = jnp.arange(TOKENS, dtype=jnp.int32)
    begins = jax.random.randint(key, (TOKENS,), 0, 256, dtype=jnp.int32) == 0
    begins = jnp.logical_or(begins, position == 0)
    begins = jnp.logical_or(begins, position == TOKENS - 1)
    return lax.cummax(jnp.where(begins, position, 0).astype(jnp.int32), axis=0)


def with_spikes(drawn, own_key, source, target, parts, factor):
    owner, partner = [(jnp.arange(drawn.shape[dim]) // (drawn.shape[dim] // parts)).reshape([-1 if axis == dim else 1 for axis in range(drawn.ndim)]) for dim in (source, target)]
    chosen = jax.random.permutation(own_key, parts)[partner]
    strong = (owner == chosen) | (owner == (partner + parts // 2) % parts)
    return jnp.where(strong, factor * drawn, drawn)


def shard_levels(own_key, dims, shards, low, top_value):
    loudness, own = 1.0, jax.random.fold_in(own_key, 6)
    for dim, blocks in shards:
        steps = jnp.exp(jax.random.uniform(jax.random.fold_in(own, dim), (blocks,), jnp.float32, low / len(shards), top_value / len(shards)))
        loudness = loudness * jnp.repeat(steps, dims[dim] // blocks).reshape([-1 if axis == dim else 1 for axis in range(len(dims))])
    return loudness


def gaussian(stream_key, extent, width, reach, shards=(), held_as=jnp.bfloat16):
    values = jax.random.normal(stream_key, extent, jnp.float32) * width
    if len(shards) > 0:
        values = shard_levels(stream_key, extent, shards, -0.22, 0.18) * values
    return jnp.clip(values, min=-reach, max=reach).astype(held_as)


def noise_with(key, shape, spread, reach, split, heavy, kind=jnp.bfloat16):
    array = spread * jax.random.normal(key, shape, jnp.float32)
    if split:
        array = array * shard_levels(key, shape, split, -0.22, 0.18)
    return jnp.clip(with_spikes(array, jax.random.fold_in(key, 3), *heavy), -reach, reach).astype(kind)


def setup_inputs(seed: int = 0) -> dict:
    key_of = jax.random.split(jax.random.key(seed), 12)
    return {
        "block_input": noise_with(key_of[0], (TOKENS, D), 1.0, 6.0, ((0, 16),), (0, 1, 16, 2.0)),
        "doc_start": draw_doc_start(jax.random.fold_in(key_of[11], 71), 0),
        "norm1_gain": jnp.clip(1.0 + 0.15 * jax.random.normal(key_of[2], (D,), jnp.float32), 0.25, 1.75).astype(jnp.bfloat16),
        "in_weight": gaussian(key_of[3], (3, D, D), D ** -0.5, 0.1875, ((1, 16), (2, 2))),
        "conv_taps": gaussian(key_of[4], (KC, D), 0.6, 3.0, ((1, 2),)),
        "out_weight": gaussian(key_of[5], (D, D), D ** -0.5, 0.1875, ((0, 2), (1, 16))),
        "norm2_gain": jnp.clip(1.0 + 0.15 * jax.random.normal(key_of[6], (D,), jnp.float32), 0.25, 1.75).astype(jnp.bfloat16),
        "gate_weight": gaussian(key_of[7], (D, FF), D ** -0.5, 0.1875, ((0, 16), (1, 2))),
        "up_weight": gaussian(key_of[8], (D, FF), D ** -0.5, 0.1875, ((0, 16), (1, 2))),
        "down_weight": gaussian(key_of[9], (FF, D), FF ** -0.5, 0.09375, ((0, 2), (1, 16))),
        "out_grad": noise_with(key_of[10], (TOKENS, D), 1.0, 6.0, ((0, 16),), (0, 1, 16, 2.0)),
    }


@jax.custom_vjp
def low(v):
    return lax.optimization_barrier(v.astype(jnp.bfloat16)).astype(jnp.float32)

@jax.custom_vjp
def low_back(v):
    return v

def low_keep(v):
    return (low(v), None)

def low_pass(kept, grad):
    return (grad,)

def back_keep(v):
    return (v, None)

def back_low(kept, grad):
    return (low(grad),)
low.defvjp(low_keep, low_pass)
low_back.defvjp(back_keep, back_low)
EPSILON = 1e-05

def matmul(first_op, second_op):
    return jnp.dot(first_op, second_op, precision=lax.Precision.HIGHEST, preferred_element_type=jnp.float32)

def rms_scale(values, gain_vec):
    factor = lax.rsqrt(lax.optimization_barrier(jnp.mean(values * values, axis=-1, keepdims=True)) + EPSILON)
    return values * factor * gain_vec

def causal_conv(mixed_rows, tap_vals, doc_start):
    length = mixed_rows.shape[0]
    position = jnp.arange(length, dtype=jnp.int32)
    result = tap_vals[0] * mixed_rows
    for offset in range(1, tap_vals.shape[0]):
        shifted = jnp.concatenate([jnp.zeros((offset, mixed_rows.shape[1]), jnp.float32), mixed_rows[:length - offset]], axis=0)
        allowed = (position - offset >= doc_start)[:, None]
        result = result + jnp.where(allowed, tap_vals[offset] * shifted, 0.0)
    return result

def forward(source, doc_start, gain_one, w_in, tap_vals, w_out, gain_two, w_gate, w_up, w_down):
    token_count = source.shape[0]
    blocks = source.reshape(token_count // TOK_DEV, TOK_DEV, D)

    def first_part(block_rows):
        normed = low(rms_scale(block_rows, gain_one))
        proj_b = low_back(matmul(normed, w_in[0]))
        proj_c = low_back(matmul(normed, w_in[1]))
        proj_x = low_back(matmul(normed, w_in[2]))
        return (low_back(low(proj_b * proj_x)), proj_c)
    mixed_rows, gate_in = lax.map(jax.checkpoint(first_part), blocks)
    conv_out = causal_conv(mixed_rows.reshape(token_count, -1), tap_vals, doc_start).reshape(mixed_rows.shape)

    def second_part(pieces):
        block_rows, gate_rows, conv_rows = pieces
        gated_rows = low(gate_rows * conv_rows)
        residual = block_rows + low_back(matmul(gated_rows, w_out))
        normed = low(rms_scale(residual, gain_two))
        gate_pre = low_back(matmul(normed, w_gate))
        up_pre = low_back(matmul(normed, w_up))
        hidden = low(jax.nn.silu(gate_pre) * up_pre)
        return residual + low_back(matmul(hidden, w_down))
    result = lax.map(jax.checkpoint(second_part), (blocks, gate_in, conv_out))
    return result.reshape(token_count, -1)

def reference(block_input, doc_start, norm1_gain, in_weight, conv_taps, out_weight, norm2_gain, gate_weight, up_weight, down_weight, out_grad):
    weight_list = tuple((weight_arr.astype(jnp.float32) for weight_arr in (norm1_gain, in_weight, conv_taps, out_weight, norm2_gain, gate_weight, up_weight, down_weight)))

    def wrapped(source, *weights):
        return forward(source, doc_start, *weights)
    output, pullback = jax.vjp(wrapped, block_input.astype(jnp.float32), *weight_list)
    grads = pullback(out_grad.astype(jnp.float32))
    return (output.astype(jnp.bfloat16), grads[0], grads[1], grads[2], grads[3], grads[4], grads[5], grads[6], grads[7], grads[8])
```

```python
import jax
import jax.numpy as jnp
from jax import lax
from jax.experimental import pallas as pl
from jax.experimental.pallas import tpu as pltpu
from jax.sharding import PartitionSpec as P

EPSILON = 1e-05
F32 = jnp.float32
BF16 = jnp.bfloat16


def shifted(value, axis, steps):
    count = lax.axis_size(axis)
    initial, last = (max(0, -steps), min(count, count - steps))
    return lax.ppermute(value, axis, [(source, source + steps) for source in range(initial, last)])


def partner(value, bits):
    return lax.ppermute(value, "seq", [(i, i ^ bits) for i in range(lax.axis_size("seq"))])


def both_cores(value):
    low = value.astype(BF16)
    return low.astype(F32) + lax.ppermute(low, "wa", [(0, 1), (1, 0)]).astype(F32)


def on_block():
    return lax.axis_size("seq") == 16 and lax.axis_size("wa") == 2


def place_kernel(own, side, ahead, corner_a, corner_b, full, buf, sems, out_sem):
    index = lax.axis_index("seq")
    z, y, x = index // 4, (index // 2) % 2, index % 2
    copies = []
    for k in range(4):
        plane = (z ^ k) * 4
        corner = corner_a if k < 2 else corner_b
        for source, row, yy, xx in (
            (own, k, y, x),
            (side, k, y, 1 - x),
            (ahead, k, 1 - y, x),
            (corner, k % 2, 1 - y, 1 - x),
        ):
            copy = pltpu.make_async_copy(
                source.at[row], buf.at[plane + yy * 2 + xx], sems.at[len(copies)]
            )
            copy.start()
            copies.append(copy)
    for copy in copies:
        copy.wait()
    last = pltpu.make_async_copy(buf, full, out_sem)
    last.start()
    last.wait()


def gather_rows(shard):
    rows, columns = shard.shape
    if not on_block():
        return lax.all_gather(shard, "seq", axis=0, tiled=True)
    own = jnp.stack([shard, partner(shard, 4), partner(shard, 8), partner(shard, 12)])
    side, ahead = partner(own, 1), partner(own, 2)
    corner_a, corner_b = partner(ahead[:2], 1), partner(side[2:], 2)
    full = pl.pallas_call(
        place_kernel,
        out_shape=jax.ShapeDtypeStruct((16, rows, columns), shard.dtype),
        in_specs=[pl.BlockSpec(memory_space=pl.ANY)] * 5,
        out_specs=pl.BlockSpec(memory_space=pl.ANY),
        scratch_shapes=[
            pltpu.VMEM((16, rows, columns), shard.dtype),
            pltpu.SemaphoreType.DMA((16,)),
            pltpu.SemaphoreType.DMA,
        ],
        compiler_params=pltpu.CompilerParams(vmem_limit_bytes=24 * 2**20),
        cost_estimate=pl.CostEstimate(flops=0, bytes_accessed=64 * rows * columns, transcendentals=0),
    )(own, side, ahead, corner_a, corner_b)
    return full.reshape(16 * rows, columns)


def scatter_rows(partial):
    if not on_block():
        return lax.psum_scatter(partial.astype(F32), "seq", scatter_dimension=0, tiled=True)
    rows, columns = partial.shape[0] // 16, partial.shape[1]
    blocks = partial.astype(BF16).reshape(4, 2, 2, rows, columns)
    index = lax.axis_index("seq")
    z, y, x = index // 4, (index // 2) % 2, index % 2

    def quarter(yy, xx):
        return lax.dynamic_slice(blocks, (0, yy, xx, 0, 0), (4, 1, 1, rows, columns)).reshape(
            4, rows, columns
        )

    corner = quarter(1 - y, 1 - x)
    from_side, from_ahead = partner(corner[:2], 1), partner(corner[2:], 2)
    ahead, side = quarter(1 - y, x), quarter(y, 1 - x)
    ahead = jnp.concatenate([(ahead[:2].astype(F32) + from_side.astype(F32)).astype(BF16), ahead[2:]])
    side = jnp.concatenate([side[:2], (side[2:].astype(F32) + from_ahead.astype(F32)).astype(BF16)])
    got_ahead, got_side = partner(ahead, 2), partner(side, 1)
    column = quarter(y, x).astype(F32) + got_ahead.astype(F32) + got_side.astype(F32)
    total = lax.dynamic_index_in_dim(column, z, 0, keepdims=False)
    for k in (1, 2, 3):
        part = lax.dynamic_index_in_dim(column, z ^ k, 0, keepdims=False).astype(BF16)
        total = total + partner(part, 4 * k).astype(F32)
    return total


def sum_all(value):
    if not on_block():
        return lax.psum(value, "seq")
    for bits in (1, 2, 4, 8):
        value = value + partner(value, bits)
    return value


def tokens_product(first_op, second_op):
    return lax.dot_general(
        first_op, second_op, (((0,), (0,)), ((), ())), preferred_element_type=F32
    )


def back_product(first_op, second_op):
    return lax.dot_general(
        first_op, second_op, (((1,), (1,)), ((), ())), preferred_element_type=F32
    )


def product(first_op, second_op):
    return jnp.dot(first_op, second_op, preferred_element_type=F32)


def local(
    block_input,
    doc_start,
    norm1_gain,
    in_weight,
    conv_taps,
    out_weight,
    norm2_gain,
    gate_weight,
    up_weight,
    down_weight,
    out_grad,
):
    row_count = block_input.shape[0]
    shard_rows, channels = in_weight.shape[1:]
    mixer_shard = jnp.concatenate(
        [in_weight[0], in_weight[1], in_weight[2], out_weight.T], axis=1
    )
    w_mixer = gather_rows(mixer_shard)
    w_gate = gather_rows(gate_weight)
    w_up = gather_rows(up_weight)
    w_down = gather_rows(down_weight.T)
    w_in, w_out = w_mixer[:, : 3 * channels], w_mixer[:, 3 * channels :]
    source = block_input.astype(F32)
    gain_one = norm1_gain.astype(F32)
    gain_two = norm2_gain.astype(F32)
    tap_vals = conv_taps.astype(F32)
    scale_one = lax.rsqrt(jnp.mean(source * source, axis=-1, keepdims=True) + EPSILON)
    hat_one = source * scale_one
    normed_in = (hat_one * gain_one).astype(BF16)
    projected = product(normed_in, w_in)
    proj_b = projected[:, :channels]
    proj_c = projected[:, channels : 2 * channels]
    proj_x = projected[:, 2 * channels :]
    mixed_rows = (proj_b * proj_x).astype(BF16)
    rim_rows = shifted(mixed_rows[row_count - 2 :], "seq", 1)
    extended = jnp.concatenate([rim_rows, mixed_rows], axis=0).astype(F32)
    mixed_now = extended[2:]
    back_one = extended[1 : row_count + 1]
    back_two = extended[:row_count]
    position = lax.axis_index("seq") * row_count + jnp.arange(row_count, dtype=jnp.int32)
    keep_one = (position - 1 >= doc_start)[:, None]
    keep_two = (position - 2 >= doc_start)[:, None]
    conv_out = (
        tap_vals[0] * mixed_now
        + jnp.where(keep_one, tap_vals[1] * back_one, 0.0)
        + jnp.where(keep_two, tap_vals[2] * back_two, 0.0)
    )
    gated_rows = (proj_c * conv_out).astype(BF16)
    mixer_out = both_cores(back_product(gated_rows, w_out))
    residual = source + mixer_out
    scale_two = lax.rsqrt(jnp.mean(residual * residual, axis=-1, keepdims=True) + EPSILON)
    hat_two = residual * scale_two
    normed_mid = (hat_two * gain_two).astype(BF16)
    gate_pre = product(normed_mid, w_gate)
    up_pre = product(normed_mid, w_up)
    sigmoid_gate = jax.nn.sigmoid(gate_pre)
    hidden = (gate_pre * sigmoid_gate * up_pre).astype(BF16)
    down_share = scatter_rows(tokens_product(out_grad, hidden))
    ffn_out = both_cores(back_product(hidden, w_down))
    block_output = (residual + ffn_out).astype(BF16)
    d_hidden = product(out_grad, w_down)
    d_up = (d_hidden * gate_pre * sigmoid_gate).astype(BF16)
    d_gate = (d_hidden * up_pre * sigmoid_gate * (1.0 + gate_pre * (1.0 - sigmoid_gate))).astype(
        BF16
    )
    gate_share = scatter_rows(tokens_product(normed_mid, d_gate))
    up_share = scatter_rows(tokens_product(normed_mid, d_up))
    d_mid = both_cores(back_product(d_gate, w_gate) + back_product(d_up, w_up))
    gain_two_grad = jnp.sum(d_mid * hat_two, axis=0)
    scaled_two = d_mid * gain_two
    d_resid = out_grad.astype(F32) + scale_two * (
        scaled_two - hat_two * jnp.mean(scaled_two * hat_two, axis=-1, keepdims=True)
    )
    d_mixer = d_resid.astype(BF16)
    mixer_grad = tokens_product(d_mixer, gated_rows)
    d_gated = product(d_mixer, w_out)
    d_conv = d_gated * proj_c
    d_proj_c = (d_gated * conv_out).astype(BF16)
    tap_grad = jnp.stack(
        [
            jnp.sum(d_conv * mixed_now, axis=0),
            jnp.sum(jnp.where(keep_one, d_conv * back_one, 0.0), axis=0),
            jnp.sum(jnp.where(keep_two, d_conv * back_two, 0.0), axis=0),
        ]
    )
    part_one = jnp.where(keep_one, tap_vals[1] * d_conv, 0.0)
    part_two = jnp.where(keep_two, tap_vals[2] * d_conv, 0.0)
    edge_rows = jnp.stack([part_two[0], part_one[0] + part_two[1]])
    incoming = shifted(edge_rows, "seq", -1)
    d_mixed = (
        tap_vals[0] * d_conv
        + jnp.concatenate([part_one[1:], jnp.zeros((1, channels), F32)], axis=0)
        + jnp.concatenate([part_two[2:], jnp.zeros((2, channels), F32)], axis=0)
        + jnp.concatenate([jnp.zeros((row_count - 2, channels), F32), incoming], axis=0)
    )
    d_mixed_low = d_mixed.astype(BF16).astype(F32)
    d_proj = jnp.concatenate(
        [
            (d_mixed_low * proj_x).astype(BF16),
            d_proj_c,
            (d_mixed_low * proj_b).astype(BF16),
        ],
        axis=1,
    )
    in_grad = tokens_product(normed_in, d_proj)
    mixer_share = scatter_rows(jnp.concatenate([in_grad, mixer_grad], axis=1))
    d_norm_in = both_cores(back_product(d_proj, w_in))
    gain_one_grad = jnp.sum(d_norm_in * hat_one, axis=0)
    scaled_one = d_norm_in * gain_one
    input_grad = d_resid + scale_one * (
        scaled_one - hat_one * jnp.mean(scaled_one * hat_one, axis=-1, keepdims=True)
    )
    width = gain_one.shape[0]
    small = jnp.concatenate(
        [gain_one_grad[None], gain_two_grad[None], jnp.pad(tap_grad, ((0, 0), (0, width - channels)))]
    )
    small = sum_all(small)
    in_share = mixer_share[:, : 3 * channels].reshape(shard_rows, 3, channels).transpose(1, 0, 2)
    return (
        block_output,
        input_grad,
        small[0],
        in_share,
        small[2:, :channels],
        mixer_share[:, 3 * channels :].T,
        small[1],
        gate_share,
        up_share,
        down_share.T,
    )


def solution(mesh):
    placed = (
        P("seq", None),
        P("seq"),
        P(),
        P(None, "seq", "wa"),
        P(None, "wa"),
        P("wa", "seq"),
        P(),
        P("seq", "wa"),
        P("seq", "wa"),
        P("wa", "seq"),
        P("seq", None),
    )
    return jax.shard_map(
        local,
        mesh=mesh,
        in_specs=placed,
        out_specs=(
            P("seq", None),
            P("seq", None),
            P(),
            P(None, "seq", "wa"),
            P(None, "wa"),
            P("wa", "seq"),
            P(),
            P("seq", "wa"),
            P("seq", "wa"),
            P("wa", "seq"),
        ),
        check_vma=False,
    )
```
